128 devices in a mesh: tm: 32 (over z, x_lo, y), head: 4 (over x_hi, core).
Axes of the slice: x: 4 (x_hi: 2, x_lo: 2; x = x_hi * 2 + x_lo), y: 4, z: 4, core: 2. Of those that a mesh axis runs over, the one named last changes fastest.
Arguments:
- queries: bfloat16 [32768, 1024], P('tm', 'head'), may hold values from -8 to 8
- keys: bfloat16 [32768, 1024], P('tm', 'head'), may hold values from -8 to 8
- values: bfloat16 [32768, 1024], P('tm', 'head'), may hold values from -6 to 6
- out_weight: bfloat16 [1024, 1024], P('head'), may hold values from -0.1875 to 0.1875
- grad_output: bfloat16 [32768, 1024], P('tm'), may hold values from -6 to 6
- tile_lists: int32 [256, 5], P('tm'), may hold values from -1 to 255, as said below
Outputs:
- output: bfloat16 [32768, 1024], P('tm', 'head')
- grad_queries: bfloat16 [32768, 1024], P('tm', 'head')
- grad_keys: bfloat16 [32768, 1024], P('tm', 'head')
- grad_values: bfloat16 [32768, 1024], P('tm', 'head')
- grad_weight: float32 [1024, 1024], P('head', 'tm')
The draws below stay inside these ranges and needn't reach their ends.
Inputs may be any that keep to these rules, and one draw needn't show every extreme that they name: `tile_lists`: the row of query tile b lists distinct key tiles t of b's recording session with b - 4 <= t <= b in falling order, the first entry b itself, then -1 in unused slots; the first tile of every stretch but the first lists the tile before it; in every draw some row uses all 5 slots.
All inputs are finite; a program needn't handle non-finite values.
Results may differ from the reference program's by a relative error of at most 0.0095.
Values may be sent and summed in bfloat16 or wider, within the bound.
No kernel may reach another device: no remote copies, remote signals or barrier semaphores. Data moves between devices by JAX's collectives and lax.ppermute only.
A program may use at most 128 MiB of HBM per device.

```python
import jax
import jax.numpy as jnp
from jax import lax

D = 1024
HEADS = 16
HD = 64
QB = 128
TOK_DEV = 1024
STRETCH = 512
CT = 4
TOKENS = 32768
N_TM = 32


def base_field(key, salt):
    subkey = jax.random.fold_in(key, salt)
    return jnp.clip(jax.random.normal(subkey, (TOKENS, D)), -6.0, 6.0)


def draw_queries(key, part):
    field = base_field(key, 11)
    return field.astype(jnp.bfloat16)


def draw_keys(key, part):
    field = base_field(key, 12)
    return field.astype(jnp.bfloat16)


def draw_tile_lists(key, part):
    blocks = TOKENS // QB
    per_piece = TOK_DEV // (2 * QB)
    reach_tiles = per_piece + 1
    devices = TOKENS // TOK_DEV
    position = jnp.arange(blocks, dtype=jnp.int32)
    piece_start = (position % per_piece == 0) & (position > 0)
    boundary = jax.random.randint(jax.random.fold_in(key, 41), (blocks,), 0, 2 * per_piece + 1) == 0
    anchor = jax.random.randint(jax.random.fold_in(key, 42), (), per_piece, blocks)
    boundary = boundary & jnp.logical_not((position > anchor - per_piece) & (position <= anchor))
    boundary = boundary & jnp.logical_not(piece_start)
    boundary = boundary | (position == 0)
    session_start = lax.cummax(jnp.where(boundary, position, 0), axis=0)
    lag_index = jnp.arange(reach_tiles, dtype=jnp.int32)
    candidate = position[:, None] - lag_index[None, :]
    kept_slot = jax.random.randint(jax.random.fold_in(key, 43), (blocks, reach_tiles), 0, 4) != 0
    kept_slot = kept_slot | (lag_index[None, :] == 0) | (position[:, None] == anchor)
    kept_slot = kept_slot | (lag_index[None, :] == 1) & piece_start[:, None]
    live_slot = kept_slot & (candidate >= session_start[:, None])
    order_key = jnp.where(live_slot, lag_index[None, :], reach_tiles + lag_index[None, :])
    slot_order = jnp.argsort(order_key, axis=1, stable=True)
    listed = jnp.take_along_axis(jnp.where(live_slot, candidate, -1), slot_order, axis=1)
    ordered = listed.reshape(2 * devices, per_piece, reach_tiles)
    stored = jnp.stack([ordered[:devices], ordered[devices:][::-1]], axis=1)
    return stored.reshape(blocks, reach_tiles).astype(jnp.int32)


def spiked(drawn, rng, source, target, blocks, factor):
    owner, partner = [(jnp.arange(drawn.shape[axis_at]) // (drawn.shape[axis_at] // blocks)).reshape([-1 if axis == axis_at else 1 for axis in range(drawn.ndim)]) for axis_at in (source, target)]
    chosen = jax.random.permutation(rng, blocks)[partner]
    strong = (owner == chosen) | (owner == (partner + blocks // 2) % blocks)
    return jnp.where(strong, factor * drawn, drawn)


def level_of(own_key, extent, cuts, smallest, largest):
    loudness = 1.0
    for dim, shards_of in cuts:
        steps = jax.random.uniform(jax.random.fold_in(jax.random.fold_in(own_key, 6), dim), (shards_of,), jnp.float32, smallest / len(cuts), largest / len(cuts))
        loudness = loudness * jnp.repeat(jnp.exp(steps), extent[dim] // shards_of).reshape((-1,) + (1,) * (len(extent) - 1 - dim))
    return loudness


def scatter_about(own_key, shape, width, bound, cuts=(), held_as=jnp.bfloat16):
    result = width * jax.random.normal(own_key, shape, jnp.float32)
    if cuts:
        result = result * level_of(own_key, shape, cuts, -0.22, 0.18)
    return jnp.clip(result, -bound, bound).astype(held_as)


def bell_draw_with(stream_key, dims, width, most, shards, heavy, held_as=jnp.bfloat16):
    values = width * jax.random.normal(stream_key, dims, jnp.float32)
    if shards:
        values = values * level_of(stream_key, dims, shards, -0.22, 0.18)
    return jnp.clip(spiked(values, jax.random.fold_in(stream_key, 3), *heavy), -most, most).astype(held_as)


def setup_inputs(seed: int = 0) -> dict:
    key_list = jax.random.split(jax.random.key(seed), 7)
    return {
        "queries": draw_queries(jax.random.fold_in(key_list[6], 71), 0),
        "keys": draw_keys(jax.random.fold_in(key_list[6], 71), 0),
        "values": scatter_about(key_list[2], (TOKENS, D), 1.0, 6.0, ((0, 32), (1, 4))),
        "out_weight": scatter_about(key_list[3], (D, D), D ** -0.5, 0.1875, ((0, 4),)),
        "grad_output": bell_draw_with(key_list[4], (TOKENS, D), 1.0, 6.0, ((0, 32),), (0, 1, 32, 2.75)),
        "tile_lists": draw_tile_lists(jax.random.fold_in(key_list[6], 71), 0),
    }


def unfold_order(stored, span_len):
    pieces = stored.reshape((N_TM, 2, span_len) + stored.shape[1:])
    return jnp.concatenate([pieces[:, 0], pieces[::-1, 1]], axis=0)


def fold_order(ordered):
    stacked = jnp.stack([ordered[:N_TM], ordered[N_TM:][::-1]], axis=1)
    return stacked.reshape((-1,) + ordered.shape[2:])


def reference(queries, keys, values, out_weight, grad_output, tile_lists):
    score_scale = HD ** -0.5
    piece_count = 2 * N_TM
    q_seq = unfold_order(queries, STRETCH).reshape(piece_count, STRETCH, HEADS, HD)
    k_seq = unfold_order(keys, STRETCH).reshape(piece_count, STRETCH, HEADS, HD)
    v_seq = unfold_order(values, STRETCH).reshape(piece_count, STRETCH, HEADS, HD)
    list_seq = unfold_order(tile_lists, CT)
    zero_piece = jnp.zeros((1, STRETCH, HEADS, HD), queries.dtype)
    k_padded = jnp.concatenate([zero_piece, k_seq], axis=0)
    v_padded = jnp.concatenate([zero_piece, v_seq], axis=0)
    piece_ids = jnp.arange(piece_count, dtype=jnp.int32)

    def window_mask(piece_id):
        tile_rows = list_seq[piece_id]
        wanted = (piece_id - 1) * CT + jnp.arange(2 * CT, dtype=jnp.int32)
        matched = (tile_rows[:, :, None] == wanted[None, None, :]) & (tile_rows[:, :, None] >= 0)
        allow_tiles = jnp.any(matched, axis=1)
        allow_tiles = jnp.repeat(jnp.repeat(allow_tiles, QB, axis=0), QB, axis=1)
        causal = jnp.arange(2 * STRETCH)[None, :] <= jnp.arange(STRETCH)[:, None] + STRETCH
        return allow_tiles & causal

    def window_keys(piece_id):
        k_here = jnp.concatenate([k_padded[piece_id], k_padded[piece_id + 1]], axis=0).astype(jnp.float32)
        v_here = jnp.concatenate([v_padded[piece_id], v_padded[piece_id + 1]], axis=0).astype(jnp.float32)
        return k_here, v_here

    def logits_of(piece_id, k_here):
        q_here = q_seq[piece_id].astype(jnp.float32)
        logits = jnp.einsum('qhd,khd->hqk', q_here, k_here) * score_scale
        return jnp.where(window_mask(piece_id)[None], logits, -1e30)

    def forward_piece(piece_id):
        k_here, v_here = window_keys(piece_id)
        logits = logits_of(piece_id, k_here)
        row_max = jnp.max(logits, axis=-1, keepdims=True)
        probability = jnp.exp(logits - row_max)
        row_total = jnp.sum(probability, axis=-1, keepdims=True)
        prob_round = lax.optimization_barrier(probability.astype(jnp.bfloat16)).astype(jnp.float32)
        mixture = jnp.einsum('hqk,khd->qhd', prob_round, v_here)
        attended = (mixture / jnp.transpose(row_total, (1, 0, 2))).astype(jnp.bfloat16)
        return attended, row_max[..., 0] + jnp.log(row_total[..., 0])

    attended_seq, log_totals = lax.map(forward_piece, piece_ids)
    attended = fold_order(attended_seq.reshape(piece_count, STRETCH, D))
    output = jnp.dot(attended, out_weight, preferred_element_type=jnp.float32).astype(jnp.bfloat16)
    grad_attn = jnp.dot(grad_output, out_weight.T, preferred_element_type=jnp.float32).astype(jnp.bfloat16)
    grad_weight = jnp.dot(attended.T, grad_output, preferred_element_type=jnp.float32) * (TOKENS ** -0.5)
    g_seq = unfold_order(grad_attn, STRETCH).reshape(piece_count, STRETCH, HEADS, HD)
    row_delta = jnp.sum(g_seq.astype(jnp.float32) * attended_seq.astype(jnp.float32), axis=-1)

    def backward_piece(piece_id):
        k_here, v_here = window_keys(piece_id)
        logits = logits_of(piece_id, k_here)
        back_prob = jnp.exp(logits - log_totals[piece_id][..., None])
        back_round = lax.optimization_barrier(back_prob.astype(jnp.bfloat16)).astype(jnp.float32)
        g_here = g_seq[piece_id].astype(jnp.float32)
        q_here = q_seq[piece_id].astype(jnp.float32)
        dv_part = jnp.einsum('hqk,qhd->khd', back_round, g_here)
        dprob = jnp.einsum('qhd,khd->hqk', g_here, v_here)
        dscore = back_prob * (dprob - jnp.transpose(row_delta[piece_id])[:, :, None])
        dscore_round = lax.optimization_barrier(dscore.astype(jnp.bfloat16)).astype(jnp.float32)
        dq_here = (jnp.einsum('hqk,khd->qhd', dscore_round, k_here) * score_scale).astype(jnp.bfloat16)
        dk_part = jnp.einsum('hqk,qhd->khd', dscore_round, q_here) * score_scale
        return dq_here, dk_part, dv_part

    dq_seq, dk_parts, dv_parts = lax.map(backward_piece, piece_ids)

    def combine(parts):
        after = jnp.concatenate([parts[1:, :STRETCH], jnp.zeros_like(parts[:1, :STRETCH])], axis=0)
        summed = (parts[:, STRETCH:] + after).astype(jnp.bfloat16)
        return fold_order(summed.reshape(piece_count, STRETCH, D))

    grad_queries = fold_order(dq_seq.reshape(piece_count, STRETCH, D))
    grad_keys = combine(dk_parts)
    grad_values = combine(dv_parts)
    return output, grad_queries, grad_keys, grad_values, grad_weight
```

```python
import jax
import jax.numpy as jnp
from jax import lax
from jax.experimental import pallas as pl
from jax.experimental.pallas import tpu as pltpu
from jax.sharding import PartitionSpec as P

HD = 64
T = 128
F32 = jnp.float32
BF16 = jnp.bfloat16


def ring(x, by):
    n = lax.axis_size("tm")
    return lax.ppermute(x, "tm", [(i, (i + by) % n) for i in range(n)])


def core_swap(x):
    return lax.ppermute(x, "head", [(0, 1), (1, 0), (2, 3), (3, 2)])


def chip_swap(x):
    return lax.ppermute(x, "head", [(0, 2), (2, 0), (1, 3), (3, 1)])


def nt(a, b):
    return lax.dot_general(a, b, (((1,), (1,)), ((), ())), preferred_element_type=F32)


def nn(a, b):
    return jnp.dot(a, b, preferred_element_type=F32)


def head_stack(x, heads):
    owner = lax.broadcasted_iota(jnp.int32, x.shape, 1) // HD
    zero = jnp.zeros_like(x)
    return jnp.concatenate([jnp.where(owner == h, x, zero) for h in range(heads)], axis=0)


def own_blocks(x, heads):
    parts = []
    for p in range(heads // 2):
        parts += [x[p][:HD, :T], x[p][HD:, T:]]
    return parts


def forward_kernel(where, lists, q, k, v, kvu, kvd, ga, att_o, p_o, g_o, del_o, kw, vt):
    width = q.shape[1]
    heads = width // HD
    span = k.shape[0] // 2
    n_tile = span // T
    reach = n_tile + 1
    last_tm = where[1] - 1
    is_last = where[0] == last_tm
    for half in range(2):
        if half == 0:
            kp, vp = kvu[:, :width], kvu[:, width:]
        else:
            kp = jnp.where(is_last, k[:span], kvd[:, :width])
            vp = jnp.where(is_last, v[:span], kvd[:, width:])
        own = pl.ds(half * span, span)
        kw[half, :span] = kp
        kw[half, span:] = k[own]
        vt[half, :, :span] = vp.T
        vt[half, :, span:] = v[own].T
    for half in range(2):
        piece = where[0] if half == 0 else 2 * where[1] - 1 - where[0]
        for j in range(n_tile):
            row = half * n_tile + j
            rows = pl.ds(row * T, T)
            win = pl.ds(j * T, reach * T)
            qm = head_stack(q[rows] * BF16(HD**-0.5), heads)
            s = nt(kw[half, win], qm)
            tiles = []
            for w in range(reach):
                t = piece * n_tile + j - n_tile + w
                hit = lists[row, 0] == t
                for c in range(1, lists.shape[1]):
                    hit = hit | (lists[row, c] == t)
                hit = hit & (t >= 0)
                sw = s[w * T : (w + 1) * T]
                ok = jnp.where(hit, 1, 0)
                if w == reach - 1:
                    key = lax.broadcasted_iota(jnp.int32, sw.shape, 0)
                    qry = lax.broadcasted_iota(jnp.int32, sw.shape, 1) % T
                    sw = jnp.where(jnp.where(key <= qry, ok, 0) > 0, sw, -1e30)
                else:
                    sw = jnp.where(ok > 0, sw, -1e30)
                tiles.append(sw)
            s = jnp.concatenate(tiles, axis=0)
            m = jnp.max(s, axis=0, keepdims=True)
            p = jnp.exp(s - m)
            inv = 1.0 / jnp.sum(p, axis=0, keepdims=True)
            pb = p.astype(BF16)
            p_o[row] = pb
            o2 = [
                nn(vt[half, 2 * HD * i : 2 * HD * (i + 1), win], pb[:, 2 * T * i : 2 * T * (i + 1)])
                for i in range(heads // 2)
            ]
            o = own_blocks(o2, heads)
            at, gt, dl = [], [], []
            for h in range(heads):
                iv = inv[:, h * T : (h + 1) * T]
                a = (o[h] * iv).astype(BF16)
                g = (ga[h * HD : (h + 1) * HD, rows] * iv).astype(BF16)
                at.append(a)
                gt.append(g)
                dl.append(jnp.sum(a.astype(F32) * g.astype(F32), axis=0, keepdims=True))
            att_o[rows] = jnp.concatenate(at, axis=0).T
            g_o[rows] = jnp.concatenate(gt, axis=0).T
            del_o[row] = jnp.concatenate(dl, axis=1)


def back_prev_kernel(where, q, k, v, kvu, kvd, p, g, dl, ret_o, dq_o, kt, acc):
    width = q.shape[1]
    heads = width // HD
    span = k.shape[0] // 2
    n_tile = span // T
    is_last = where[0] == where[1] - 1
    for half in range(2):
        if half == 0:
            kp, vp = kvu[:, :width], kvu[:, width:]
        else:
            kp = jnp.where(is_last, k[:span], kvd[:, :width])
            vp = jnp.where(is_last, v[:span], kvd[:, width:])
        kt[...] = kp.T
        for j in range(n_tile):
            row = half * n_tile + j
            rows = pl.ds(row * T, T)
            size = span - j * T
            gm = head_stack(g[rows], heads)
            qm = head_stack(q[rows] * BF16(HD**-0.5), heads)
            pb = p[row, :size]
            dp = nt(vp[j * T :], gm)
            ds = (pb.astype(F32) * (dp - dl[row])).astype(BF16)
            d2 = [
                nn(kt[2 * HD * i : 2 * HD * (i + 1), j * T :], ds[:, 2 * T * i : 2 * T * (i + 1)])
                for i in range(heads // 2)
            ]
            dq_o[:, rows] = jnp.concatenate(own_blocks(d2, heads), axis=0)
            dk, dv = nn(ds, qm), nn(pb, gm)
            if j == 0:
                acc[:, :width] = dk
                acc[:, width:] = dv
            else:
                acc[j * T :, :width] += dk
                acc[j * T :, width:] += dv
        ret_o[half] = acc[...].astype(BF16)


def back_own_kernel(q, k, v, p, g, dl, dqp, dq_o, dk_o, dv_o, kt):
    width = q.shape[1]
    heads = width // HD
    span = k.shape[0] // 2
    n_tile = span // T
    for half in range(2):
        own = half * span
        kt[...] = k[own : own + span].T
        for j in reversed(range(n_tile)):
            row = half * n_tile + j
            rows = pl.ds(row * T, T)
            size = (j + 1) * T
            gm = head_stack(g[rows], heads)
            qm = head_stack(q[rows] * BF16(HD**-0.5), heads)
            pb = p[row, span - j * T :]
            dp = nt(v[own : own + size], gm)
            ds = (pb.astype(F32) * (dp - dl[row])).astype(BF16)
            d2 = [
                nn(kt[2 * HD * i : 2 * HD * (i + 1), :size], ds[:, 2 * T * i : 2 * T * (i + 1)])
                for i in range(heads // 2)
            ]
            dq = jnp.concatenate(own_blocks(d2, heads), axis=0) + dqp[:, rows]
            dq_o[rows] = (dq * HD**-0.5).astype(BF16).T
            dk, dv = nn(ds, qm), nn(pb, gm)
            if j == n_tile - 1:
                dk_o[own : own + size] = dk
                dv_o[own : own + size] = dv
            else:
                dk_o[own : own + size] += dk
                dv_o[own : own + size] += dv


def call(body, outs, scratch, scalars, flops, *args):
    vm = pl.BlockSpec(memory_space=pltpu.VMEM)
    sm = pl.BlockSpec(memory_space=pltpu.SMEM)
    return pl.pallas_call(
        body,
        out_shape=outs,
        in_specs=[sm] * scalars + [vm] * (len(args) - scalars),
        out_specs=[vm] * len(outs),
        scratch_shapes=scratch,
        compiler_params=pltpu.CompilerParams(vmem_limit_bytes=56 << 20),
        cost_estimate=pl.CostEstimate(flops=flops, transcendentals=0, bytes_accessed=8 << 20),
    )(*args)


def on_device(queries, keys, values, out_weight, grad_output, tile_lists):
    rows, width = queries.shape
    heads = width // HD
    span = rows // 2
    n_tile = span // T
    n_row = 2 * n_tile
    tm_count = lax.axis_size("tm")
    tm_index = lax.axis_index("tm")
    head_index = lax.axis_index("head")
    shape = jax.ShapeDtypeStruct
    is_last = tm_index == tm_count - 1
    where = jnp.stack([tm_index, jnp.int32(tm_count)]).astype(jnp.int32)

    kv = jnp.concatenate([keys, values], axis=1)
    kvu = ring(kv[:span], 1)
    kvd = ring(kv[span:], -1)

    w4 = out_weight.reshape(width, 2, 2, width)
    core = head_index % 2
    chip = head_index // 2
    w_core = lax.dynamic_index_in_dim(w4, core, axis=2, keepdims=False)
    w_send = lax.dynamic_index_in_dim(w4, 1 - core, axis=2, keepdims=False)
    w_recv = core_swap(w_send.reshape(width, 2 * width)).reshape(width, 2, width)

    ga = lax.dot_general(out_weight, grad_output, (((1,), (1,)), ((), ())), preferred_element_type=F32)

    att, p, g, dl = call(
        forward_kernel,
        [
            shape((rows, width), BF16),
            shape((n_row, (n_tile + 1) * T, heads * T), BF16),
            shape((rows, width), BF16),
            shape((n_row, 1, heads * T), F32),
        ],
        [pltpu.VMEM((2, 2 * span, width), BF16), pltpu.VMEM((2, width, 2 * span), BF16)],
        2,
        4 * 10**9,
        where,
        tile_lists,
        queries,
        keys,
        values,
        kvu,
        kvd,
        ga,
    )

    att_other = core_swap(att)
    wt = lax.dot_general(grad_output, att, (((0,), (0,)), ((), ())), preferred_element_type=F32)
    there = lax.dynamic_index_in_dim(w_core, 1 - chip, axis=1, keepdims=False)
    there_o = lax.dynamic_index_in_dim(w_recv, 1 - chip, axis=1, keepdims=False)
    here = lax.dynamic_index_in_dim(w_core, chip, axis=1, keepdims=False)
    here_o = lax.dynamic_index_in_dim(w_recv, chip, axis=1, keepdims=False)
    out_recv = chip_swap((nn(att, there) + nn(att_other, there_o)).astype(BF16))

    ret, dqp = call(
        back_prev_kernel,
        [shape((2, span, 2 * width), BF16), shape((width, rows), F32)],
        [pltpu.VMEM((width, span), BF16), pltpu.VMEM((span, 2 * width), F32)],
        1,
        4 * 10**9,
        where,
        queries,
        keys,
        values,
        kvu,
        kvd,
        p,
        g,
        dl,
    )
    back_low = ring(ret[0], -1)
    back_high = ring(ret[1], 1)

    w_split = wt.astype(BF16).reshape(tm_count, -1, width)
    w_parts = lax.all_to_all(w_split, "tm", 0, 0, tiled=True)

    dq, dk, dv = call(
        back_own_kernel,
        [shape((rows, width), BF16), shape((rows, width), F32), shape((rows, width), F32)],
        [pltpu.VMEM((width, span), BF16)],
        0,
        4 * 10**9,
        queries,
        keys,
        values,
        p,
        g,
        dl,
        dqp,
    )
    output = (nn(att, here) + nn(att_other, here_o) + out_recv.astype(F32)).astype(BF16)
    low = jnp.where(is_last, ret[1], back_low).astype(F32)
    high = jnp.where(tm_index == 0, jnp.zeros_like(back_high), back_high).astype(F32)
    halo = jnp.concatenate([low, high], axis=0)
    grad_keys = (dk + halo[:, :width]).astype(BF16)
    grad_values = (dv + halo[:, width:]).astype(BF16)
    scale = (tm_count * rows) ** -0.5
    grad_weight = (jnp.sum(w_parts.astype(F32), axis=0) * scale).T
    return output, dq, grad_keys, grad_values, grad_weight


def solution(mesh):
    return jax.shard_map(
        on_device,
        mesh=mesh,
        in_specs=(
            P("tm", "head"),
            P("tm", "head"),
            P("tm", "head"),
            P("head", None),
            P("tm", None),
            P("tm", None),
        ),
        out_specs=(
            P("tm", "head"),
            P("tm", "head"),
            P("tm", "head"),
            P("tm", "head"),
            P("head", "tm"),
        ),
        check_vma=False,
    )
```

```python
import jax
import jax.numpy as jnp
from jax import lax
from jax.experimental import pallas as pl
from jax.experimental.pallas import tpu as pltpu
from jax.sharding import PartitionSpec as P

HD = 64
T = 128
F32 = jnp.float32
BF16 = jnp.bfloat16


def ring(x, by):
    n = lax.axis_size("tm")
    return lax.ppermute(x, "tm", [(i, (i + by) % n) for i in range(n)])


def core_swap(x):
    return lax.ppermute(x, "head", [(0, 1), (1, 0), (2, 3), (3, 2)])


def chip_swap(x):
    return lax.ppermute(x, "head", [(0, 2), (2, 0), (1, 3), (3, 1)])


def nt(a, b):
    return lax.dot_general(a, b, (((1,), (1,)), ((), ())), preferred_element_type=F32)


def nn(a, b):
    return jnp.dot(a, b, preferred_element_type=F32)


def pair_stack(x):
    first = lax.broadcasted_iota(jnp.int32, x.shape, 1) < HD
    zero = jnp.zeros_like(x)
    return jnp.concatenate([jnp.where(first, x, zero), jnp.where(first, zero, x)], axis=0)


def own_blocks(x):
    return jnp.concatenate([x[:HD, :T], x[HD:, T:]], axis=0)


def per_head(r):
    return jnp.concatenate(
        [jnp.broadcast_to(r[:, :T], (HD, T)), jnp.broadcast_to(r[:, T:], (HD, T))], axis=0
    )


def head_sums(x):
    return jnp.concatenate(
        [jnp.sum(x[:HD], axis=0, keepdims=True), jnp.sum(x[HD:], axis=0, keepdims=True)], axis=1
    )


def listed(lists, row, tile):
    hit = lists[row, 0] == tile
    for c in range(1, lists.shape[1]):
        hit = hit | (lists[row, c] == tile)
    return jnp.where(hit & (tile >= 0), 1, 0)


def masked_max(s, oks, start):
    m = start
    for w, ok in enumerate(oks):
        mw = jnp.max(s[w * T : (w + 1) * T], axis=0, keepdims=True)
        mw = jnp.where(ok > 0, mw, -1e30)
        m = mw if m is None else jnp.maximum(m, mw)
    return m


def masked_exp(s, oks, m):
    parts, total = [], None
    for w, ok in enumerate(oks):
        p = jnp.exp(s[w * T : (w + 1) * T] - jnp.where(ok > 0, m, 1e30))
        t = jnp.sum(p, axis=0, keepdims=True)
        total = t if total is None else total + t
        parts.append(p.astype(BF16))
    return jnp.concatenate(parts, axis=0), total


def first_tile(where, half, n_tile):
    return (where[0] if half == 0 else 2 * where[1] - 1 - where[0]) * n_tile


def staged(items, stages):
    held = [dict() for _ in items]
    for step in range(len(items) + len(stages) - 1):
        for lag, stage in enumerate(stages):
            if 0 <= step - lag < len(items):
                stage(held[step - lag], *items[step - lag])


def chains(pairs, n_tile):
    return [(half, j, i) for half in range(2) for j in range(n_tile) for i in range(pairs)]


def lanes(i):
    return slice(2 * HD * i, 2 * HD * (i + 1))


def cols(j):
    return slice(2 * T * j, 2 * T * (j + 1))


def own_forward_kernel(where, lists, q, k, v, p_o, st_o, o_o, vt):
    pairs = q.shape[1] // (2 * HD)
    span = k.shape[0] // 2
    n_tile = span // T
    vt[...] = v[...].T
    key = lax.broadcasted_iota(jnp.int32, (T, 2 * T), 0)
    qry = lax.broadcasted_iota(jnp.int32, (T, 2 * T), 1) % T
    causal = key <= qry
    tile0 = [first_tile(where, half, n_tile) for half in range(2)]
    oks = [
        [[listed(lists, half * n_tile + j, tile0[half] + w) for w in range(j + 1)] for j in range(n_tile)]
        for half in range(2)
    ]

    def scores(d, half, j, i):
        lo = half * span
        row = lo + j * T
        qm = pair_stack(q[row : row + T, lanes(i)] * BF16(HD**-0.5))
        s = nt(k[lo : row + T, lanes(i)], qm)
        diag = jnp.where(causal, s[j * T :], -1e30)
        d["s"] = diag if j == 0 else jnp.concatenate([s[: j * T], diag], axis=0)

    def softmax(d, half, j, i):
        row = half * n_tile + j
        m = masked_max(d["s"], oks[half][j], None)
        d["p"], total = masked_exp(d.pop("s"), oks[half][j], m)
        p_o[half, i, : (j + 1) * T, cols(j)] = d["p"]
        st_o[row, 0:1, cols(i)] = m
        st_o[row, 1:2, cols(i)] = total

    def mix(d, half, j, i):
        lo = half * span
        row = lo + j * T
        o_o[lanes(i), row : row + T] = own_blocks(nn(vt[lanes(i), lo : row + T], d.pop("p")))

    staged(chains(pairs, n_tile), [scores, softmax, mix])


def halo_kernel(
    where, lists, q, k, v, kvu, kvd, ga, st, o1, att_o, attt_o, g_o, del_o, ret_o, dq_o, kp, vp, kt, vt, ps, ds, qs, gs
):
    pairs = q.shape[1] // (2 * HD)
    span = k.shape[0] // 2
    n_tile = span // T
    is_last = where[0] == where[1] - 1
    for half in range(2):
        if half == 0:
            kp[half] = kvu[:span]
            vp[half] = kvu[span:]
        else:
            kp[half] = jnp.where(is_last, k[:span], kvd[:span])
            vp[half] = jnp.where(is_last, v[:span], kvd[span:])
        kt[half] = kp[half].T
        vt[half] = vp[half].T
    tile0 = [first_tile(where, half, n_tile) - n_tile for half in range(2)]
    oks = [
        [[listed(lists, half * n_tile + j, tile0[half] + w) for w in range(j, n_tile)] for j in range(n_tile)]
        for half in range(2)
    ]

    def scores(d, half, j, i):
        row = half * span + j * T
        qm = pair_stack(q[row : row + T, lanes(i)] * BF16(HD**-0.5))
        qs[half, i, cols(j)] = qm
        d["s"] = nt(kp[half, j * T :, lanes(i)], qm)

    def softmax(d, half, j, i):
        row = half * n_tile + j
        m1 = st[row, 0:1, cols(i)]
        m = masked_max(d["s"], oks[half][j], m1)
        d["alpha"] = jnp.exp(m1 - m)
        d["p"], total = masked_exp(d.pop("s"), oks[half][j], m)
        ps[half, i, j * T :, cols(j)] = d["p"]
        d["inv"] = 1.0 / (d["alpha"] * st[row, 1:2, cols(i)] + total)

    def mix(d, half, j, i):
        d["o"] = own_blocks(nn(vt[half, lanes(i), j * T :], d.pop("p")))

    def finish(d, half, j, i):
        row = half * n_tile + j
        rows = slice(row * T, (row + 1) * T)
        alpha, inv = d.pop("alpha"), d.pop("inv")
        at = ((o1[lanes(i), rows] * per_head(alpha) + d.pop("o")) * per_head(inv)).astype(BF16)
        gh = ga[lanes(i), rows]
        g2 = (gh * per_head(inv)).astype(BF16)
        g1 = (gh * per_head(inv * alpha)).astype(BF16)
        af = at.astype(F32)
        d["d2"] = head_sums(af * g2.astype(F32))
        del_o[row, :, cols(i)] = head_sums(af * g1.astype(F32))
        attt_o[lanes(i), rows] = at
        att_o[rows, lanes(i)] = at.T
        g_o[rows, lanes(i)] = g1.T
        d["gm"] = pair_stack(g2.T)
        gs[half, i, cols(j)] = d["gm"]

    def dprob(d, half, j, i):
        d["dp"] = nt(vp[half, j * T :, lanes(i)], d.pop("gm"))

    def dscore(d, half, j, i):
        p = ps[half, i, j * T :, cols(j)].astype(F32)
        ds[half, i, j * T :, cols(j)] = (p * (d.pop("dp") - d.pop("d2"))).astype(BF16)

    def gradients(half):
        for i in range(pairs):
            for t in range(n_tile):
                upto = slice(0, 2 * T * (t + 1))
                tile = slice(t * T, (t + 1) * T)
                ret_o[half, tile, lanes(i)] = nn(ds[half, i, tile, upto], qs[half, i, upto]).astype(BF16)
                back = slice(span + t * T, span + (t + 1) * T)
                ret_o[half, back, lanes(i)] = nn(ps[half, i, tile, upto], gs[half, i, upto]).astype(BF16)
            for j in range(n_tile):
                row = half * span + j * T
                dq_o[lanes(i), row : row + T] = own_blocks(
                    nn(kt[half, lanes(i), j * T :], ds[half, i, j * T :, cols(j)])
                )

    staged(chains(pairs, n_tile), [scores, softmax, mix, finish, dprob, dscore])
    for half in range(2):
        gradients(half)


def own_back_kernel(where, q, k, v, p, g, dl, dqp, ret, low, high, dq_o, dk_o, dv_o, kt, ds, qs, gs):
    pairs = q.shape[1] // (2 * HD)
    span = k.shape[0] // 2
    n_tile = span // T
    is_last = where[0] == where[1] - 1
    is_first = where[0] == 0
    kt[...] = k[...].T

    def dprob(d, half, j, i):
        lo = half * span
        row = lo + j * T
        gm = pair_stack(g[row : row + T, lanes(i)])
        gs[half, i, cols(j)] = gm
        qs[half, i, cols(j)] = pair_stack(q[row : row + T, lanes(i)] * BF16(HD**-0.5))
        d["dp"] = nt(v[lo : row + T, lanes(i)], gm)

    def dscore(d, half, j, i):
        size = (j + 1) * T
        pf = p[half, i, :size, cols(j)].astype(F32)
        ds[half, i, :size, cols(j)] = (pf * (d.pop("dp") - dl[half * n_tile + j, :, cols(i)])).astype(BF16)

    def gradients(half):
        lo = half * span
        for i in range(pairs):
            for t in range(n_tile):
                since = slice(2 * T * t, 2 * T * n_tile)
                tile = slice(t * T, (t + 1) * T)
                there = slice(span + t * T, span + (t + 1) * T)
                rows = slice(lo + t * T, lo + (t + 1) * T)
                dk = nn(ds[half, i, tile, since], qs[half, i, since])
                dv = nn(p[half, i, tile, since], gs[half, i, since])
                if half == 0:
                    hk = jnp.where(is_last, ret[1, tile, lanes(i)], low[tile, lanes(i)])
                    hv = jnp.where(is_last, ret[1, there, lanes(i)], low[there, lanes(i)])
                else:
                    hk, hv = high[tile, lanes(i)], high[there, lanes(i)]
                    hk = jnp.where(is_first, jnp.zeros_like(hk), hk)
                    hv = jnp.where(is_first, jnp.zeros_like(hv), hv)
                dk_o[rows, lanes(i)] = (dk + hk.astype(F32)).astype(BF16)
                dv_o[rows, lanes(i)] = (dv + hv.astype(F32)).astype(BF16)
            for j in range(n_tile):
                rows = slice(lo + j * T, lo + (j + 1) * T)
                dq = own_blocks(nn(kt[lanes(i), lo : lo + (j + 1) * T], ds[half, i, : (j + 1) * T, cols(j)]))
                dq_o[rows, lanes(i)] = ((dq + dqp[lanes(i), rows]) * HD**-0.5).astype(BF16).T

    staged(chains(pairs, n_tile), [dprob, dscore])
    for half in range(2):
        gradients(half)


def weight_kernel(at, go, w_o):
    w_o[...] = nn(at[...], go[...]).astype(BF16).T


def call(body, outs, scratch, scalars, flops, *args):
    vm = pl.BlockSpec(memory_space=pltpu.VMEM)
    sm = pl.BlockSpec(memory_space=pltpu.SMEM)
    return pl.pallas_call(
        body,
        out_shape=outs,
        in_specs=[sm] * scalars + [vm] * (len(args) - scalars),
        out_specs=[vm] * len(outs),
        scratch_shapes=scratch,
        compiler_params=pltpu.CompilerParams(vmem_limit_bytes=56 << 20),
        cost_estimate=pl.CostEstimate(flops=flops, transcendentals=0, bytes_accessed=8 << 20),
    )(*args)


def on_device(queries, keys, values, out_weight, grad_output, tile_lists):
    rows, width = queries.shape
    heads = width // HD
    span = rows // 2
    n_tile = span // T
    n_row = 2 * n_tile
    tm_count = lax.axis_size("tm")
    tm_index = lax.axis_index("tm")
    head_index = lax.axis_index("head")
    where = jnp.stack([tm_index, jnp.int32(tm_count)]).astype(jnp.int32)

    def arr(dtype, *dims):
        return jax.ShapeDtypeStruct(dims, dtype)

    def vmem(dtype, *dims):
        return pltpu.VMEM(dims, dtype)

    kvu = ring(jnp.concatenate([keys[:span], values[:span]], axis=0), 1)
    kvd = ring(jnp.concatenate([keys[span:], values[span:]], axis=0), -1)

    w4 = out_weight.reshape(width, 2, 2, width)
    core = head_index % 2
    chip = head_index // 2
    w_core = lax.dynamic_index_in_dim(w4, core, axis=2, keepdims=False)
    w_send = lax.dynamic_index_in_dim(w4, 1 - core, axis=2, keepdims=False)
    w_recv = core_swap(w_send.reshape(width, 2 * width)).reshape(width, 2, width)

    ga = lax.dot_general(out_weight, grad_output, (((1,), (1,)), ((), ())), preferred_element_type=F32)

    p, st, o1 = call(
        own_forward_kernel,
        [arr(BF16, 2, heads // 2, span, 2 * span), arr(F32, n_row, 2, heads * T), arr(F32, width, rows)],
        [vmem(BF16, width, rows)],
        2,
        10**9,
        where,
        tile_lists,
        queries,
        keys,
        values,
    )
    att, at, g, dl, ret, dqp = call(
        halo_kernel,
        [
            arr(BF16, rows, width),
            arr(BF16, width, rows),
            arr(BF16, rows, width),
            arr(F32, n_row, 1, heads * T),
            arr(BF16, 2, rows, width),
            arr(F32, width, rows),
        ],
        [vmem(BF16, 2, span, width)] * 2
        + [vmem(BF16, 2, width, span)] * 2
        + [vmem(BF16, 2, heads // 2, span, 2 * span)] * 2
        + [vmem(BF16, 2, heads // 2, 2 * span, 2 * HD)] * 2,
        2,
        4 * 10**9,
        where,
        tile_lists,
        queries,
        keys,
        values,
        kvu,
        kvd,
        ga,
        st,
        o1,
    )
    low = ring(ret[0], -1)
    high = ring(ret[1], 1)

    att_other = core_swap(att)
    (w_mine,) = call(weight_kernel, [arr(BF16, grad_output.shape[1], width)], [], 0, 10**9, at, grad_output)
    there = lax.dynamic_index_in_dim(w_core, 1 - chip, axis=1, keepdims=False)
    there_o = lax.dynamic_index_in_dim(w_recv, 1 - chip, axis=1, keepdims=False)
    here = lax.dynamic_index_in_dim(w_core, chip, axis=1, keepdims=False)
    here_o = lax.dynamic_index_in_dim(w_recv, chip, axis=1, keepdims=False)
    out_recv = chip_swap((nn(att, there) + nn(att_other, there_o)).astype(BF16))
    w_parts = lax.all_to_all(w_mine.reshape(tm_count, -1, width), "tm", 0, 0, tiled=True)

    dq, dk, dv = call(
        own_back_kernel,
        [arr(BF16, rows, width)] * 3,
        [vmem(BF16, width, rows), vmem(BF16, 2, heads // 2, span, 2 * span)]
        + [vmem(BF16, 2, heads // 2, 2 * span, 2 * HD)] * 2,
        1,
        4 * 10**9,
        where,
        queries,
        keys,
        values,
        p,
        g,
        dl,
        dqp,
        ret,
        low,
        high,
    )
    output = (nn(att, here) + nn(att_other, here_o) + out_recv.astype(F32)).astype(BF16)
    scale = (tm_count * rows) ** -0.5
    grad_weight = (jnp.sum(w_parts.astype(F32), axis=0) * scale).T
    return output, dq, dk, dv, grad_weight


def solution(mesh):
    return jax.shard_map(
        on_device,
        mesh=mesh,
        in_specs=(
            P("tm", "head"),
            P("tm", "head"),
            P("tm", "head"),
            P("head", None),
            P("tm", None),
            P("tm", None),
        ),
        out_specs=(
            P("tm", "head"),
            P("tm", "head"),
            P("tm", "head"),
            P("tm", "head"),
            P("head", "tm"),
        ),
        check_vma=False,
    )
```

```python
import jax
import jax.numpy as jnp
from jax import lax
from jax.experimental import pallas as pl
from jax.experimental.pallas import tpu as pltpu
from jax.sharding import PartitionSpec as P

HD = 64
T = 128
F32 = jnp.float32
BF16 = jnp.bfloat16


def ring(x, by):
    n = lax.axis_size("tm")
    return lax.ppermute(x, "tm", [(i, (i + by) % n) for i in range(n)])


def core_swap(x):
    return lax.ppermute(x, "head", [(0, 1), (1, 0), (2, 3), (3, 2)])


def chip_swap(x):
    return lax.ppermute(x, "head", [(0, 2), (2, 0), (1, 3), (3, 1)])


def nt(a, b):
    return lax.dot_general(a, b, (((1,), (1,)), ((), ())), preferred_element_type=F32)


def nn(a, b):
    return jnp.dot(a, b, preferred_element_type=F32)


def pair_stack(x):
    first = lax.broadcasted_iota(jnp.int32, x.shape, 1) < HD
    zero = jnp.zeros_like(x)
    return jnp.concatenate([jnp.where(first, x, zero), jnp.where(first, zero, x)], axis=0)


def own_blocks(x):
    return jnp.concatenate([x[:HD, :T], x[HD:, T:]], axis=0)


def per_head(r):
    return jnp.concatenate(
        [jnp.broadcast_to(r[:, :T], (HD, T)), jnp.broadcast_to(r[:, T:], (HD, T))], axis=0
    )


def head_sums(x):
    return jnp.concatenate(
        [jnp.sum(x[:HD], axis=0, keepdims=True), jnp.sum(x[HD:], axis=0, keepdims=True)], axis=1
    )


def listed(lists, row, tile):
    hit = lists[row, 0] == tile
    for c in range(1, lists.shape[1]):
        hit = hit | (lists[row, c] == tile)
    return jnp.where(hit & (tile >= 0), 1, 0)


def masked_max(s, oks, start):
    m = start
    for w, ok in enumerate(oks):
        mw = jnp.max(s[w * T : (w + 1) * T], axis=0, keepdims=True)
        mw = jnp.where(ok > 0, mw, -1e30)
        m = mw if m is None else jnp.maximum(m, mw)
    return m


def masked_exp(s, oks, m):
    parts, total = [], None
    for w, ok in enumerate(oks):
        p = jnp.exp(s[w * T : (w + 1) * T] - jnp.where(ok > 0, m, 1e30))
        t = jnp.sum(p, axis=0, keepdims=True)
        total = t if total is None else total + t
        parts.append(p.astype(BF16))
    return jnp.concatenate(parts, axis=0), total


def first_tile(where, half, n_tile):
    return (where[0] if half == 0 else 2 * where[1] - 1 - where[0]) * n_tile


def staged(items, stages):
    held = [dict() for _ in items]
    for step in range(len(items) + len(stages) - 1):
        for lag, stage in enumerate(stages):
            if 0 <= step - lag < len(items):
                stage(held[step - lag], *items[step - lag])


def chains(pairs, n_tile):
    return [(half, j, i) for half in range(2) for j in range(n_tile) for i in range(pairs)]


def lanes(i):
    return slice(2 * HD * i, 2 * HD * (i + 1))


def cols(j):
    return slice(2 * T * j, 2 * T * (j + 1))


def own_forward_kernel(where, lists, q, k, v, p_o, st_o, o_o, vt):
    pairs = q.shape[1] // (2 * HD)
    span = k.shape[0] // 2
    n_tile = span // T
    vt[...] = v[...].T
    key = lax.broadcasted_iota(jnp.int32, (T, 2 * T), 0)
    qry = lax.broadcasted_iota(jnp.int32, (T, 2 * T), 1) % T
    causal = key <= qry
    tile0 = [first_tile(where, half, n_tile) for half in range(2)]
    oks = [
        [[listed(lists, half * n_tile + j, tile0[half] + w) for w in range(j + 1)] for j in range(n_tile)]
        for half in range(2)
    ]

    def scores(d, half, j, i):
        lo = half * span
        row = lo + j * T
        qm = pair_stack(q[row : row + T, lanes(i)] * BF16(HD**-0.5))
        s = nt(k[lo : row + T, lanes(i)], qm)
        diag = jnp.where(causal, s[j * T :], -1e30)
        d["s"] = diag if j == 0 else jnp.concatenate([s[: j * T], diag], axis=0)

    def softmax(d, half, j, i):
        row = half * n_tile + j
        m = masked_max(d["s"], oks[half][j], None)
        d["p"], total = masked_exp(d.pop("s"), oks[half][j], m)
        p_o[half, i, : (j + 1) * T, cols(j)] = d["p"]
        st_o[row, 0:1, cols(i)] = m
        st_o[row, 1:2, cols(i)] = total

    def mix(d, half, j, i):
        lo = half * span
        row = lo + j * T
        o_o[lanes(i), row : row + T] = own_blocks(nn(vt[lanes(i), lo : row + T], d.pop("p")))

    staged(chains(pairs, n_tile), [scores, softmax, mix])


def halo_kernel(
    where, lists, q, k, v, kvu, kvd, ga, st, o1, att_o, attt_o, g_o, del_o, low_o, high_o, dq_o, kp, vp, kt, vt, ps, ds, qs, gs
):
    pairs = q.shape[1] // (2 * HD)
    span = k.shape[0] // 2
    n_tile = span // T
    is_last = where[0] == where[1] - 1
    for half in range(2):
        if half == 0:
            kp[half] = kvu[:span]
            vp[half] = kvu[span:]
        else:
            kp[half] = jnp.where(is_last, k[:span], kvd[:span])
            vp[half] = jnp.where(is_last, v[:span], kvd[span:])
        kt[half] = kp[half].T
        vt[half] = vp[half].T
    tile0 = [first_tile(where, half, n_tile) - n_tile for half in range(2)]
    oks = [
        [[listed(lists, half * n_tile + j, tile0[half] + w) for w in range(j, n_tile)] for j in range(n_tile)]
        for half in range(2)
    ]

    def scores(d, half, j, i):
        row = half * span + j * T
        qm = pair_stack(q[row : row + T, lanes(i)] * BF16(HD**-0.5))
        qs[half, i, cols(j)] = qm
        d["s"] = nt(kp[half, j * T :, lanes(i)], qm)

    def softmax(d, half, j, i):
        row = half * n_tile + j
        m1 = st[row, 0:1, cols(i)]
        m = masked_max(d["s"], oks[half][j], m1)
        d["alpha"] = jnp.exp(m1 - m)
        d["p"], total = masked_exp(d.pop("s"), oks[half][j], m)
        ps[half, i, j * T :, cols(j)] = d["p"]
        d["inv"] = 1.0 / (d["alpha"] * st[row, 1:2, cols(i)] + total)

    def mix(d, half, j, i):
        d["o"] = own_blocks(nn(vt[half, lanes(i), j * T :], d.pop("p")))

    def finish(d, half, j, i):
        row = half * n_tile + j
        rows = slice(row * T, (row + 1) * T)
        alpha, inv = d.pop("alpha"), d.pop("inv")
        at = ((o1[lanes(i), rows] * per_head(alpha) + d.pop("o")) * per_head(inv)).astype(BF16)
        gh = ga[lanes(i), rows]
        g2 = (gh * per_head(inv)).astype(BF16)
        g1 = (gh * per_head(inv * alpha)).astype(BF16)
        af = at.astype(F32)
        d["d2"] = head_sums(af * g2.astype(F32))
        del_o[row, :, cols(i)] = head_sums(af * g1.astype(F32))
        attt_o[lanes(i), rows] = at
        att_o[rows, lanes(i)] = at.T
        g_o[rows, lanes(i)] = g1.T
        d["gm"] = pair_stack(g2.T)
        gs[half, i, cols(j)] = d["gm"]

    def dprob(d, half, j, i):
        d["dp"] = nt(vp[half, j * T :, lanes(i)], d.pop("gm"))

    def dscore(d, half, j, i):
        p = ps[half, i, j * T :, cols(j)].astype(F32)
        ds[half, i, j * T :, cols(j)] = (p * (d.pop("dp") - d.pop("d2"))).astype(BF16)

    def gradients(half):
        ret_o = low_o if half == 0 else high_o
        for i in range(pairs):
            for t in range(n_tile):
                upto = slice(0, 2 * T * (t + 1))
                tile = slice(t * T, (t + 1) * T)
                ret_o[tile, lanes(i)] = nn(ds[half, i, tile, upto], qs[half, i, upto]).astype(BF16)
                back = slice(span + t * T, span + (t + 1) * T)
                ret_o[back, lanes(i)] = nn(ps[half, i, tile, upto], gs[half, i, upto]).astype(BF16)
            for j in range(n_tile):
                row = half * span + j * T
                dq_o[lanes(i), row : row + T] = own_blocks(
                    nn(kt[half, lanes(i), j * T :], ds[half, i, j * T :, cols(j)])
                )

    staged(chains(pairs, n_tile), [scores, softmax, mix, finish, dprob, dscore])
    for half in range(2):
        gradients(half)


def own_back_kernel(where, q, k, v, p, g, dl, dqp, ret, low, high, dq_o, dk_o, dv_o, kt, ds, qs, gs):
    pairs = q.shape[1] // (2 * HD)
    span = k.shape[0] // 2
    n_tile = span // T
    is_last = where[0] == where[1] - 1
    is_first = where[0] == 0
    kt[...] = k[...].T

    def dprob(d, half, j, i):
        lo = half * span
        row = lo + j * T
        gm = pair_stack(g[row : row + T, lanes(i)])
        gs[half, i, cols(j)] = gm
        qs[half, i, cols(j)] = pair_stack(q[row : row + T, lanes(i)] * BF16(HD**-0.5))
        d["dp"] = nt(v[lo : row + T, lanes(i)], gm)

    def dscore(d, half, j, i):
        size = (j + 1) * T
        pf = p[half, i, :size, cols(j)].astype(F32)
        ds[half, i, :size, cols(j)] = (pf * (d.pop("dp") - dl[half * n_tile + j, :, cols(i)])).astype(BF16)

    def gradients(half):
        lo = half * span
        for i in range(pairs):
            for t in range(n_tile):
                since = slice(2 * T * t, 2 * T * n_tile)
                tile = slice(t * T, (t + 1) * T)
                there = slice(span + t * T, span + (t + 1) * T)
                rows = slice(lo + t * T, lo + (t + 1) * T)
                dk = nn(ds[half, i, tile, since], qs[half, i, since])
                dv = nn(p[half, i, tile, since], gs[half, i, since])
                if half == 0:
                    hk = jnp.where(is_last, ret[tile, lanes(i)], low[tile, lanes(i)])
                    hv = jnp.where(is_last, ret[there, lanes(i)], low[there, lanes(i)])
                else:
                    hk, hv = high[tile, lanes(i)], high[there, lanes(i)]
                    hk = jnp.where(is_first, jnp.zeros_like(hk), hk)
                    hv = jnp.where(is_first, jnp.zeros_like(hv), hv)
                dk_o[rows, lanes(i)] = (dk + hk.astype(F32)).astype(BF16)
                dv_o[rows, lanes(i)] = (dv + hv.astype(F32)).astype(BF16)
            for j in range(n_tile):
                rows = slice(lo + j * T, lo + (j + 1) * T)
                dq = own_blocks(nn(kt[lanes(i), lo : lo + (j + 1) * T], ds[half, i, : (j + 1) * T, cols(j)]))
                dq_o[rows, lanes(i)] = ((dq + dqp[lanes(i), rows]) * HD**-0.5).astype(BF16).T

    staged(chains(pairs, n_tile), [dprob, dscore])
    for half in range(2):
        gradients(half)


def weight_kernel(at, go, w_o):
    w_o[...] = nn(at[...], go[...]).astype(BF16).T


def call(body, outs, scratch, scalars, flops, *args):
    vm = pl.BlockSpec(memory_space=pltpu.VMEM)
    sm = pl.BlockSpec(memory_space=pltpu.SMEM)
    return pl.pallas_call(
        body,
        out_shape=outs,
        in_specs=[sm] * scalars + [vm] * (len(args) - scalars),
        out_specs=[vm] * len(outs),
        scratch_shapes=scratch,
        compiler_params=pltpu.CompilerParams(vmem_limit_bytes=56 << 20),
        cost_estimate=pl.CostEstimate(flops=flops, transcendentals=0, bytes_accessed=8 << 20),
    )(*args)


def on_device(queries, keys, values, out_weight, grad_output, tile_lists):
    rows, width = queries.shape
    heads = width // HD
    span = rows // 2
    n_tile = span // T
    n_row = 2 * n_tile
    tm_count = lax.axis_size("tm")
    tm_index = lax.axis_index("tm")
    head_index = lax.axis_index("head")
    where = jnp.stack([tm_index, jnp.int32(tm_count)]).astype(jnp.int32)

    def arr(dtype, *dims):
        return jax.ShapeDtypeStruct(dims, dtype)

    def vmem(dtype, *dims):
        return pltpu.VMEM(dims, dtype)

    kvu = ring(jnp.concatenate([keys[:span], values[:span]], axis=0), 1)
    kvd = ring(jnp.concatenate([keys[span:], values[span:]], axis=0), -1)

    ga = lax.dot_general(out_weight, grad_output, (((1,), (1,)), ((), ())), preferred_element_type=F32)

    p, st, o1 = call(
        own_forward_kernel,
        [arr(BF16, 2, heads // 2, span, 2 * span), arr(F32, n_row, 2, heads * T), arr(F32, width, rows)],
        [vmem(BF16, width, rows)],
        2,
        10**9,
        where,
        tile_lists,
        queries,
        keys,
        values,
    )
    st, weight = lax.optimization_barrier((st, out_weight))
    w4 = weight.reshape(width, 2, 2, width)
    core = head_index % 2
    chip = head_index // 2
    w_core = lax.dynamic_index_in_dim(w4, core, axis=2, keepdims=False)
    w_send = lax.dynamic_index_in_dim(w4, 1 - core, axis=2, keepdims=False)
    w_recv = core_swap(w_send.reshape(width, 2 * width)).reshape(width, 2, width)
    there = lax.dynamic_index_in_dim(w_core, 1 - chip, axis=1, keepdims=False)
    there_o = lax.dynamic_index_in_dim(w_recv, 1 - chip, axis=1, keepdims=False)
    here = lax.dynamic_index_in_dim(w_core, chip, axis=1, keepdims=False)
    here_o = lax.dynamic_index_in_dim(w_recv, chip, axis=1, keepdims=False)
    st, here, here_o, there, there_o = lax.optimization_barrier((st, here, here_o, there, there_o))
    att, at, g, dl, ret_low, ret_high, dqp = call(
        halo_kernel,
        [
            arr(BF16, rows, width),
            arr(BF16, width, rows),
            arr(BF16, rows, width),
            arr(F32, n_row, 1, heads * T),
            arr(BF16, rows, width),
            arr(BF16, rows, width),
            arr(F32, width, rows),
        ],
        [vmem(BF16, 2, span, width)] * 2
        + [vmem(BF16, 2, width, span)] * 2
        + [vmem(BF16, 2, heads // 2, span, 2 * span)] * 2
        + [vmem(BF16, 2, heads // 2, 2 * span, 2 * HD)] * 2,
        2,
        4 * 10**9,
        where,
        tile_lists,
        queries,
        keys,
        values,
        kvu,
        kvd,
        ga,
        st,
        o1,
    )
    low = ring(ret_low, -1)
    high = ring(ret_high, 1)

    att_other = core_swap(att)
    at, att_other = lax.optimization_barrier((at, att_other))
    (w_mine,) = call(weight_kernel, [arr(BF16, grad_output.shape[1], width)], [], 0, 10**9, at, grad_output)
    out_recv = chip_swap((nn(att, there) + nn(att_other, there_o)).astype(BF16))
    w_parts = lax.all_to_all(w_mine.reshape(tm_count, -1, width), "tm", 0, 0, tiled=True)

    dq, dk, dv = call(
        own_back_kernel,
        [arr(BF16, rows, width)] * 3,
        [vmem(BF16, width, rows), vmem(BF16, 2, heads // 2, span, 2 * span)]
        + [vmem(BF16, 2, heads // 2, 2 * span, 2 * HD)] * 2,
        1,
        4 * 10**9,
        where,
        queries,
        keys,
        values,
        p,
        g,
        dl,
        dqp,
        ret_high,
        low,
        high,
    )
    output = (nn(att, here) + nn(att_other, here_o) + out_recv.astype(F32)).astype(BF16)
    scale = (tm_count * rows) ** -0.5
    grad_weight = (jnp.sum(w_parts.astype(F32), axis=0) * scale).T
    return output, dq, dk, dv, grad_weight


def solution(mesh):
    return jax.shard_map(
        on_device,
        mesh=mesh,
        in_specs=(
            P("tm", "head"),
            P("tm", "head"),
            P("tm", "head"),
            P("head", None),
            P("tm", None),
            P("tm", None),
        ),
        out_specs=(
            P("tm", "head"),
            P("tm", "head"),
            P("tm", "head"),
            P("tm", "head"),
            P("head", "tm"),
        ),
        check_vma=False,
    )
```

```python
import jax
import jax.numpy as jnp
from jax import lax
from jax.experimental import pallas as pl
from jax.experimental.pallas import tpu as pltpu
from jax.sharding import PartitionSpec as P

HD = 64
T = 128
F32 = jnp.float32
BF16 = jnp.bfloat16


def ring(x, by):
    n = lax.axis_size("tm")
    return lax.ppermute(x, "tm", [(i, (i + by) % n) for i in range(n)])


def core_swap(x):
    return lax.ppermute(x, "head", [(0, 1), (1, 0), (2, 3), (3, 2)])


def chip_swap(x):
    return lax.ppermute(x, "head", [(0, 2), (2, 0), (1, 3), (3, 1)])


def nt(a, b):
    return lax.dot_general(a, b, (((1,), (1,)), ((), ())), preferred_element_type=F32)


def nn(a, b):
    return jnp.dot(a, b, preferred_element_type=F32)


def pair_stack(x):
    first = lax.broadcasted_iota(jnp.int32, x.shape, 1) < HD
    zero = jnp.zeros_like(x)
    return jnp.concatenate([jnp.where(first, x, zero), jnp.where(first, zero, x)], axis=0)


def own_blocks(x):
    return jnp.concatenate([x[:HD, :T], x[HD:, T:]], axis=0)


def per_head(r):
    return jnp.concatenate(
        [jnp.broadcast_to(r[:, :T], (HD, T)), jnp.broadcast_to(r[:, T:], (HD, T))], axis=0
    )


def head_sums(x):
    return jnp.concatenate(
        [jnp.sum(x[:HD], axis=0, keepdims=True), jnp.sum(x[HD:], axis=0, keepdims=True)], axis=1
    )


def listed(lists, row, tile):
    hit = lists[row, 0] == tile
    for c in range(1, lists.shape[1]):
        hit = hit | (lists[row, c] == tile)
    return jnp.where(hit & (tile >= 0), 1, 0)


def masked_max(s, oks, start):
    m = start
    for w, ok in enumerate(oks):
        mw = jnp.max(s[w * T : (w + 1) * T], axis=0, keepdims=True)
        mw = jnp.where(ok > 0, mw, -1e30)
        m = mw if m is None else jnp.maximum(m, mw)
    return m


def masked_exp(s, oks, m):
    parts, total = [], None
    for w, ok in enumerate(oks):
        p = jnp.exp(s[w * T : (w + 1) * T] - jnp.where(ok > 0, m, 1e30))
        t = jnp.sum(p, axis=0, keepdims=True)
        total = t if total is None else total + t
        parts.append(p.astype(BF16))
    return jnp.concatenate(parts, axis=0), total


def first_tile(where, half, n_tile):
    return (where[0] if half == 0 else 2 * lax.axis_size("tm") - 1 - where[0]) * n_tile


def staged(items, stages):
    held = [dict() for _ in items]
    for step in range(len(items) + len(stages) - 1):
        for lag, stage in enumerate(stages):
            if 0 <= step - lag < len(items):
                stage(held[step - lag], *items[step - lag])


def chains(pairs, n_tile):
    return [(half, j, i) for half in range(2) for j in range(n_tile) for i in range(pairs)]


def lanes(i):
    return slice(2 * HD * i, 2 * HD * (i + 1))


def cols(j):
    return slice(2 * T * j, 2 * T * (j + 1))


def own_forward_kernel(where, lists, q, k, v, p_o, st_o, o_o, vt):
    pairs = q.shape[1] // (2 * HD)
    span = k.shape[0] // 2
    n_tile = span // T
    vt[...] = v[...].T
    key = lax.broadcasted_iota(jnp.int32, (T, 2 * T), 0)
    qry = lax.broadcasted_iota(jnp.int32, (T, 2 * T), 1) % T
    causal = key <= qry
    tile0 = [first_tile(where, half, n_tile) for half in range(2)]
    oks = [
        [[listed(lists, half * n_tile + j, tile0[half] + w) for w in range(j + 1)] for j in range(n_tile)]
        for half in range(2)
    ]

    def scores(d, half, j, i):
        lo = half * span
        row = lo + j * T
        qm = pair_stack(q[row : row + T, lanes(i)] * BF16(HD**-0.5))
        s = nt(k[lo : row + T, lanes(i)], qm)
        diag = jnp.where(causal, s[j * T :], -1e30)
        d["s"] = diag if j == 0 else jnp.concatenate([s[: j * T], diag], axis=0)

    def softmax(d, half, j, i):
        row = half * n_tile + j
        m = masked_max(d["s"], oks[half][j], None)
        d["p"], total = masked_exp(d.pop("s"), oks[half][j], m)
        p_o[half, i, : (j + 1) * T, cols(j)] = d["p"]
        st_o[row, 0:1, cols(i)] = m
        st_o[row, 1:2, cols(i)] = total

    def mix(d, half, j, i):
        lo = half * span
        row = lo + j * T
        o_o[lanes(i), row : row + T] = own_blocks(nn(vt[lanes(i), lo : row + T], d.pop("p")))

    staged(chains(pairs, n_tile), [scores, softmax, mix])


def halo_kernel(
    where, lists, q, k, v, kvu, kvd, ga, st, o1, att_o, attt_o, g_o, del_o, low_o, high_o, dq_o, kp, vp, kt, vt, ps, ds, qs, gs
):
    pairs = q.shape[1] // (2 * HD)
    span = k.shape[0] // 2
    n_tile = span // T
    is_last = where[0] == lax.axis_size("tm") - 1
    for half in range(2):
        if half == 0:
            kp[half] = kvu[:span]
            vp[half] = kvu[span:]
        else:
            kp[half] = jnp.where(is_last, k[:span], kvd[:span])
            vp[half] = jnp.where(is_last, v[:span], kvd[span:])
        kt[half] = kp[half].T
        vt[half] = vp[half].T
    tile0 = [first_tile(where, half, n_tile) - n_tile for half in range(2)]
    oks = [
        [[listed(lists, half * n_tile + j, tile0[half] + w) for w in range(j, n_tile)] for j in range(n_tile)]
        for half in range(2)
    ]

    def scores(d, half, j, i):
        row = half * span + j * T
        qm = pair_stack(q[row : row + T, lanes(i)] * BF16(HD**-0.5))
        qs[half, i, cols(j)] = qm
        d["s"] = nt(kp[half, j * T :, lanes(i)], qm)

    def softmax(d, half, j, i):
        row = half * n_tile + j
        m1 = st[row, 0:1, cols(i)]
        m = masked_max(d["s"], oks[half][j], m1)
        d["alpha"] = jnp.exp(m1 - m)
        d["p"], total = masked_exp(d.pop("s"), oks[half][j], m)
        ps[half, i, j * T :, cols(j)] = d["p"]
        d["inv"] = 1.0 / (d["alpha"] * st[row, 1:2, cols(i)] + total)

    def mix(d, half, j, i):
        d["o"] = own_blocks(nn(vt[half, lanes(i), j * T :], d.pop("p")))

    def finish(d, half, j, i):
        row = half * n_tile + j
        rows = slice(row * T, (row + 1) * T)
        alpha, inv = d.pop("alpha"), d.pop("inv")
        at = ((o1[lanes(i), rows] * per_head(alpha) + d.pop("o")) * per_head(inv)).astype(BF16)
        gh = ga[lanes(i), rows]
        g2 = (gh * per_head(inv)).astype(BF16)
        g1 = (gh * per_head(inv * alpha)).astype(BF16)
        af = at.astype(F32)
        d["d2"] = head_sums(af * g2.astype(F32))
        del_o[row, :, cols(i)] = head_sums(af * g1.astype(F32))
        attt_o[lanes(i), rows] = at
        att_o[rows, lanes(i)] = at.T
        g_o[rows, lanes(i)] = g1.T
        d["gm"] = pair_stack(g2.T)
        gs[half, i, cols(j)] = d["gm"]

    def dprob(d, half, j, i):
        d["dp"] = nt(vp[half, j * T :, lanes(i)], d.pop("gm"))

    def dscore(d, half, j, i):
        p = ps[half, i, j * T :, cols(j)].astype(F32)
        ds[half, i, j * T :, cols(j)] = (p * (d.pop("dp") - d.pop("d2"))).astype(BF16)

    def gradients(half):
        ret_o = low_o if half == 0 else high_o
        for i in range(pairs):
            for t in range(n_tile):
                upto = slice(0, 2 * T * (t + 1))
                tile = slice(t * T, (t + 1) * T)
                ret_o[tile, lanes(i)] = nn(ds[half, i, tile, upto], qs[half, i, upto]).astype(BF16)
                back = slice(span + t * T, span + (t + 1) * T)
                ret_o[back, lanes(i)] = nn(ps[half, i, tile, upto], gs[half, i, upto]).astype(BF16)
            for j in range(n_tile):
                row = half * span + j * T
                dq_o[lanes(i), row : row + T] = own_blocks(
                    nn(kt[half, lanes(i), j * T :], ds[half, i, j * T :, cols(j)])
                )

    staged(chains(pairs, n_tile), [scores, softmax, mix, finish, dprob, dscore])
    for half in range(2):
        gradients(half)


def own_back_kernel(where, q, k, v, p, g, dl, dqp, ret, low, high, dq_o, dk_o, dv_o, kt, ds, qs, gs):
    pairs = q.shape[1] // (2 * HD)
    span = k.shape[0] // 2
    n_tile = span // T
    is_last = where[0] == lax.axis_size("tm") - 1
    is_first = where[0] == 0
    kt[...] = k[...].T

    def dprob(d, half, j, i):
        lo = half * span
        row = lo + j * T
        gm = pair_stack(g[row : row + T, lanes(i)])
        gs[half, i, cols(j)] = gm
        qs[half, i, cols(j)] = pair_stack(q[row : row + T, lanes(i)] * BF16(HD**-0.5))
        d["dp"] = nt(v[lo : row + T, lanes(i)], gm)

    def dscore(d, half, j, i):
        size = (j + 1) * T
        pf = p[half, i, :size, cols(j)].astype(F32)
        ds[half, i, :size, cols(j)] = (pf * (d.pop("dp") - dl[half * n_tile + j, :, cols(i)])).astype(BF16)

    def gradients(half):
        lo = half * span
        for i in range(pairs):
            for t in range(n_tile):
                since = slice(2 * T * t, 2 * T * n_tile)
                tile = slice(t * T, (t + 1) * T)
                there = slice(span + t * T, span + (t + 1) * T)
                rows = slice(lo + t * T, lo + (t + 1) * T)
                dk = nn(ds[half, i, tile, since], qs[half, i, since])
                dv = nn(p[half, i, tile, since], gs[half, i, since])
                if half == 0:
                    hk = jnp.where(is_last, ret[tile, lanes(i)], low[tile, lanes(i)])
                    hv = jnp.where(is_last, ret[there, lanes(i)], low[there, lanes(i)])
                else:
                    hk, hv = high[tile, lanes(i)], high[there, lanes(i)]
                    hk = jnp.where(is_first, jnp.zeros_like(hk), hk)
                    hv = jnp.where(is_first, jnp.zeros_like(hv), hv)
                dk_o[rows, lanes(i)] = (dk + hk.astype(F32)).astype(BF16)
                dv_o[rows, lanes(i)] = (dv + hv.astype(F32)).astype(BF16)
            for j in range(n_tile):
                rows = slice(lo + j * T, lo + (j + 1) * T)
                dq = own_blocks(nn(kt[lanes(i), lo : lo + (j + 1) * T], ds[half, i, : (j + 1) * T, cols(j)]))
                dq_o[rows, lanes(i)] = ((dq + dqp[lanes(i), rows]) * HD**-0.5).astype(BF16).T

    staged(chains(pairs, n_tile), [dprob, dscore])
    for half in range(2):
        gradients(half)


def weight_kernel(at, go, w_o):
    w_o[...] = nn(at[...], go[...]).astype(BF16).T


def call(body, outs, scratch, scalars, flops, *args):
    vm = pl.BlockSpec(memory_space=pltpu.VMEM)
    sm = pl.BlockSpec(memory_space=pltpu.SMEM)
    return pl.pallas_call(
        body,
        out_shape=outs,
        in_specs=[sm] * scalars + [vm] * (len(args) - scalars),
        out_specs=[vm] * len(outs),
        scratch_shapes=scratch,
        compiler_params=pltpu.CompilerParams(vmem_limit_bytes=56 << 20),
        cost_estimate=pl.CostEstimate(flops=flops, transcendentals=0, bytes_accessed=8 << 20),
    )(*args)


def on_device(queries, keys, values, out_weight, grad_output, tile_lists):
    rows, width = queries.shape
    heads = width // HD
    span = rows // 2
    n_tile = span // T
    n_row = 2 * n_tile
    tm_count = lax.axis_size("tm")
    tm_index = lax.axis_index("tm")
    head_index = lax.axis_index("head")
    where = tm_index.astype(jnp.int32).reshape(1)

    def arr(dtype, *dims):
        return jax.ShapeDtypeStruct(dims, dtype)

    def vmem(dtype, *dims):
        return pltpu.VMEM(dims, dtype)

    kvu = ring(jnp.concatenate([keys[:span], values[:span]], axis=0), 1)
    kvd = ring(jnp.concatenate([keys[span:], values[span:]], axis=0), -1)

    w4 = out_weight.reshape(width, 2, 2, width)
    core = head_index % 2
    chip = head_index // 2
    w_core = lax.dynamic_index_in_dim(w4, core, axis=2, keepdims=False)
    w_send = lax.dynamic_index_in_dim(w4, 1 - core, axis=2, keepdims=False)
    w_recv = core_swap(w_send.reshape(width, 2 * width)).reshape(width, 2, width)

    ga = lax.dot_general(out_weight, grad_output, (((1,), (1,)), ((), ())), preferred_element_type=F32)

    p, st, o1 = call(
        own_forward_kernel,
        [arr(BF16, 2, heads // 2, span, 2 * span), arr(F32, n_row, 2, heads * T), arr(F32, width, rows)],
        [vmem(BF16, width, rows)],
        2,
        10**9,
        where,
        tile_lists,
        queries,
        keys,
        values,
    )
    att, at, g, dl, ret_low, ret_high, dqp = call(
        halo_kernel,
        [
            arr(BF16, rows, width),
            arr(BF16, width, rows),
            arr(BF16, rows, width),
            arr(F32, n_row, 1, heads * T),
            arr(BF16, rows, width),
            arr(BF16, rows, width),
            arr(F32, width, rows),
        ],
        [vmem(BF16, 2, span, width)] * 2
        + [vmem(BF16, 2, width, span)] * 2
        + [vmem(BF16, 2, heads // 2, span, 2 * span)] * 2
        + [vmem(BF16, 2, heads // 2, 2 * span, 2 * HD)] * 2,
        2,
        4 * 10**9,
        where,
        tile_lists,
        queries,
        keys,
        values,
        kvu,
        kvd,
        ga,
        st,
        o1,
    )
    low = ring(ret_low, -1)
    high = ring(ret_high, 1)

    att_other = core_swap(att)
    at, att_other = lax.optimization_barrier((at, att_other))
    (w_mine,) = call(weight_kernel, [arr(BF16, grad_output.shape[1], width)], [], 0, 10**9, at, grad_output)
    there = lax.dynamic_index_in_dim(w_core, 1 - chip, axis=1, keepdims=False)
    there_o = lax.dynamic_index_in_dim(w_recv, 1 - chip, axis=1, keepdims=False)
    here = lax.dynamic_index_in_dim(w_core, chip, axis=1, keepdims=False)
    here_o = lax.dynamic_index_in_dim(w_recv, chip, axis=1, keepdims=False)
    out_recv = chip_swap((nn(att, there) + nn(att_other, there_o)).astype(BF16))
    w_parts = lax.all_to_all(w_mine.reshape(tm_count, -1, width), "tm", 0, 0, tiled=True)

    dq, dk, dv = call(
        own_back_kernel,
        [arr(BF16, rows, width)] * 3,
        [vmem(BF16, width, rows), vmem(BF16, 2, heads // 2, span, 2 * span)]
        + [vmem(BF16, 2, heads // 2, 2 * span, 2 * HD)] * 2,
        1,
        4 * 10**9,
        where,
        queries,
        keys,
        values,
        p,
        g,
        dl,
        dqp,
        ret_high,
        low,
        high,
    )
    output = (nn(att, here) + nn(att_other, here_o) + out_recv.astype(F32)).astype(BF16)
    scale = (tm_count * rows) ** -0.5
    grad_weight = (jnp.sum(w_parts.astype(F32), axis=0) * scale).T
    return output, dq, dk, dv, grad_weight


def solution(mesh):
    return jax.shard_map(
        on_device,
        mesh=mesh,
        in_specs=(
            P("tm", "head"),
            P("tm", "head"),
            P("tm", "head"),
            P("head", None),
            P("tm", None),
            P("tm", None),
        ),
        out_specs=(
            P("tm", "head"),
            P("tm", "head"),
            P("tm", "head"),
            P("tm", "head"),
            P("head", "tm"),
        ),
        check_vma=False,
    )
```
